32 devices in a mesh: energy: 8 (over y, x, core), layer: 4 (over z).
Axes of the slice: x: 2, y: 2, z: 4, core: 2. Of those that a mesh axis runs over, the one named last changes fastest.
Arguments:
- green: bfloat16 [256, 4, 256, 256], P('energy', 'layer'), may hold values from -6 to 6
- gradient: bfloat16 [4, 256, 256], P('layer'), may hold values from -0.375 to 0.375
- left_coupling: bfloat16 [4, 256, 128], P('layer'), may hold values from -0.5 to 0.5
- right_coupling: bfloat16 [4, 256, 128], P('layer'), may hold values from -0.5 to 0.5
- dynamical: float32 [4, 256, 256], P('layer'), may hold values from -0.2 to 3
- omega_sq: float32 [8], replicated, may hold values from 1 to 4
- shifts: int32 [8], replicated, may hold values from 1 to 32, as said below
Outputs:
- phonon_self: float32 [8, 4, 256, 256], P('energy', 'layer')
- phonon_green: float32 [8, 4, 256, 256], P('energy', 'layer')
- electron_self: bfloat16 [256, 4, 256, 256], P('energy', 'layer')
The draws below stay inside these ranges and needn't reach their ends.
Inputs may be any that keep to these rules, and one draw needn't show every extreme that they name: `shifts`: the largest shift is 32.
All inputs are finite; a program needn't handle non-finite values.
Results may differ from the reference program's by a relative error of at most 0.017.
Values may be sent and summed in bfloat16 or wider, within the bound.
No kernel may reach another device: no remote copies, remote signals or barrier semaphores. Data moves between devices by JAX's collectives and lax.ppermute only.
A program may use at most 192 MiB of HBM per device.

```python
import math
import jax
import jax.numpy as jnp
from jax import lax

NB = 256
BND = 128
E_DEV = 32
NEWTON = 3
NE = 256
LAYERS = 4
W = 8


def draw_dynamical(key, part):
    halves = jax.random.split(key, 2)
    log_diag = jax.random.uniform(halves[0], (LAYERS, NB), jnp.float32, 0.0, math.log(3.0))
    diagonal = jnp.exp(log_diag)
    spread = jnp.clip(0.03 * jax.random.normal(halves[1], (LAYERS, NB, NB), jnp.float32), -0.2, 0.2)
    identity = jnp.eye(NB, dtype=jnp.float32)
    return spread * (1.0 - identity) + diagonal[:, :, None] * identity


def draw_shifts(key, part):
    values = jax.random.randint(key, (W,), 1, E_DEV + 1)
    position = jax.random.randint(jax.random.fold_in(key, 7), (), 0, W)
    return values.at[position].set(E_DEV).astype(jnp.int32)


def shard_levels(stream_key, extent, cuts, low, largest):
    def one(dim, parts):
        draws = jax.random.uniform(jax.random.fold_in(jax.random.fold_in(stream_key, 6), dim), (parts,), jnp.float32, low / len(cuts), largest / len(cuts))
        return jnp.repeat(jnp.exp(draws), extent[dim] // parts).reshape((-1,) + (1,) * (len(extent) - dim - 1))

    factor_of = one(*cuts[0])
    for cut in cuts[1:]:
        factor_of = factor_of * one(*cut)
    return factor_of


def centred(stream_key, dims, scale, bound, shards=(), kind=jnp.bfloat16):
    entries = jax.random.normal(stream_key, dims, jnp.float32) * scale
    if len(shards) > 0:
        entries = shard_levels(stream_key, dims, shards, -0.22, 0.18) * entries
    return jnp.clip(entries, min=-bound, max=bound).astype(kind)


def setup_inputs(seed: int = 0) -> dict:
    key_of = jax.random.split(jax.random.key(seed), 8)
    green = centred(key_of[0], (NE, LAYERS, NB, NB), 1.0, 6.0, ((0, 8), (1, 4)))
    gradient = centred(key_of[1], (LAYERS, NB, NB), NB ** -0.5, 0.375, ((0, 4),))
    left_coupling = centred(key_of[2], (LAYERS, NB, BND), BND ** -0.5, 0.5, ((0, 4),))
    right_coupling = centred(key_of[3], (LAYERS, NB, BND), BND ** -0.5, 0.5, ((0, 4),))
    dynamical = draw_dynamical(jax.random.fold_in(key_of[7], 71), 0)
    omega_sq = jnp.clip(jnp.exp(jax.random.uniform(key_of[5], (W,), jnp.float32, math.log(1.0), math.log(4.0))), 1.0, 4.0)
    shifts = draw_shifts(jax.random.fold_in(key_of[7], 71), 0)
    return {"green": green, "gradient": gradient, "left_coupling": left_coupling, "right_coupling": right_coupling, "dynamical": dynamical, "omega_sq": omega_sq, "shifts": shifts}


coupling = 0.01

def invert(matrix):
    identity = jnp.eye(matrix.shape[-1], dtype=jnp.float32)
    diagonal = jnp.diagonal(matrix, axis1=1, axis2=2)
    approx = identity[None] / diagonal[:, None, :]
    for repeat in range(NEWTON):
        product = jnp.einsum('kij,kjl->kil', matrix, approx, precision=lax.Precision.HIGHEST)
        approx = 2.0 * approx - jnp.einsum('kij,kjl->kil', approx, product, precision=lax.Precision.HIGHEST)
    return approx

def reference(green, gradient, left_coupling, right_coupling, dynamical, omega_sq, shifts):
    zero_blocks = jnp.zeros((NE, 1, BND, BND), jnp.bfloat16)
    from_left = jnp.concatenate([zero_blocks, green[:, :-1, NB - BND:, NB - BND:]], axis=1)
    from_right = jnp.concatenate([green[:, 1:, :BND, :BND], zero_blocks], axis=1)
    energies = jnp.arange(NE, dtype=jnp.int32)
    scale = 1.0 / math.sqrt(NE)

    def one_layer(inputs):
        blocks, layer_grad, left_cpl, right_cpl, left_in, right_in, stiffness = inputs
        grad_wide = layer_grad.astype(jnp.float32)
        first_half = jnp.einsum('ij,ejk->eik', grad_wide, blocks.astype(jnp.float32)).astype(jnp.bfloat16)
        summed = jnp.einsum('eij,kj->eik', first_half.astype(jnp.float32), grad_wide)
        left_part = jnp.einsum('ij,ejk->eik', left_cpl.astype(jnp.float32), left_in.astype(jnp.float32)).astype(jnp.bfloat16)
        summed = summed + jnp.einsum('eij,kj->eik', left_part.astype(jnp.float32), left_cpl.astype(jnp.float32))
        right_part = jnp.einsum('ij,ejk->eik', right_cpl.astype(jnp.float32), right_in.astype(jnp.float32)).astype(jnp.bfloat16)
        summed = summed + jnp.einsum('eij,kj->eik', right_part.astype(jnp.float32), right_cpl.astype(jnp.float32))
        sandwich = summed.astype(jnp.bfloat16)
        sandwich_wide = sandwich.astype(jnp.float32)

        def phonon_term(offset):
            upward = energies + offset
            inside = (upward < NE).astype(jnp.float32)
            slices = blocks[jnp.minimum(upward, NE - 1)].astype(jnp.float32) * inside[:, None, None]
            return lax.optimization_barrier(jnp.sum(sandwich_wide * slices, axis=0)) * scale
        phonon_self = lax.map(phonon_term, shifts)
        identity = jnp.eye(NB, dtype=jnp.float32)
        matrix = stiffness[None] + omega_sq[:, None, None] * identity[None] + coupling * phonon_self
        phonon_green = invert(matrix)
        rounded = phonon_green.astype(jnp.bfloat16)

        def add_term(running, paired):
            green_one, offset = paired
            downward = energies - offset
            inside = (downward >= 0).astype(jnp.float32)
            slices = sandwich_wide[jnp.maximum(downward, 0)] * inside[:, None, None]
            return (running + green_one.astype(jnp.float32)[None] * slices, None)
        mixture, unused = lax.scan(add_term, jnp.zeros((NE, NB, NB), jnp.float32), (rounded, shifts))
        mixture = mixture.astype(jnp.bfloat16)
        second = jnp.einsum('ij,ejk->eik', grad_wide, mixture.astype(jnp.float32)).astype(jnp.bfloat16)
        electron = jnp.einsum('eij,kj->eik', second.astype(jnp.float32), grad_wide).astype(jnp.bfloat16)
        return (phonon_self, phonon_green, electron)
    layered = (jnp.moveaxis(green, 1, 0), gradient, left_coupling, right_coupling, jnp.moveaxis(from_left, 1, 0), jnp.moveaxis(from_right, 1, 0), dynamical)
    self_all, green_all, electron_all = lax.map(one_layer, layered)
    return (jnp.moveaxis(self_all, 0, 1), jnp.moveaxis(green_all, 0, 1), jnp.moveaxis(electron_all, 0, 1))
```

```python
import functools
import math

import jax
import jax.numpy as jnp
from jax import lax
from jax.experimental import pallas as pl
from jax.experimental.pallas import tpu as pltpu
from jax.sharding import PartitionSpec as P

NEWTON = 3
coupling = 0.01
F32 = jnp.float32
BF16 = jnp.bfloat16
ANY = pl.BlockSpec(memory_space=pl.ANY)
VMEM = pl.BlockSpec(memory_space=pltpu.VMEM)
SMEM = pl.BlockSpec(memory_space=pltpu.SMEM)


def shifted(value, axis, steps):
    count = lax.axis_size(axis)
    leading, last = (max(0, -steps), min(count, count - steps))
    return lax.ppermute(value, axis, [(source, source + steps) for source in range(leading, last)])


def partner(value, axis, mask):
    count = lax.axis_size(axis)
    return lax.ppermute(value, axis, [(source, source ^ mask) for source in range(count)])


def dot_nn(a, b):
    return lax.dot_general(a, b, (((1,), (0,)), ((), ())), preferred_element_type=F32)


def dot_nt(a, b):
    return lax.dot_general(a, b, (((1,), (1,)), ((), ())), preferred_element_type=F32)


def sandwich_kernel(g_ref, l_ref, r_ref, grad_ref, lc_ref, rc_ref, out_ref):
    count, order = g_ref.shape[0], g_ref.shape[-1]
    surface = l_ref.shape[-1]
    grad, lc, rc = grad_ref[...], lc_ref[...], rc_ref[...]
    tg = dot_nt(g_ref[...].reshape(count * order, order), grad).astype(BF16)
    tl = dot_nt(l_ref[...].reshape(count * surface, surface), lc).astype(BF16)
    tr = dot_nt(r_ref[...].reshape(count * surface, surface), rc).astype(BF16)
    for e in range(count):
        total = dot_nn(grad, tg[e * order : (e + 1) * order])
        total = total + dot_nn(lc, tl[e * surface : (e + 1) * surface])
        total = total + dot_nn(rc, tr[e * surface : (e + 1) * surface])
        out_ref[e] = total.astype(BF16)


def sandwich_of(green, first, count, left_in, right_in, grad, lc, rc, step):
    order = green.shape[-1]
    surface = left_in.shape[-1]
    base = first // step
    flops = 2 * count * (2 * order**3 + 2 * surface**2 * order + 2 * surface * order**2)
    return pl.pallas_call(
        sandwich_kernel,
        grid=(count // step,),
        in_specs=[
            pl.BlockSpec((step, None, order, order), lambda i: (base + i, 0, 0, 0)),
            pl.BlockSpec((step, surface, surface), lambda i: (i, 0, 0)),
            pl.BlockSpec((step, surface, surface), lambda i: (i, 0, 0)),
            pl.BlockSpec((None, order, order), lambda i: (0, 0, 0)),
            pl.BlockSpec((None, order, surface), lambda i: (0, 0, 0)),
            pl.BlockSpec((None, order, surface), lambda i: (0, 0, 0)),
        ],
        out_specs=pl.BlockSpec((step, order, order), lambda i: (i, 0, 0)),
        out_shape=jax.ShapeDtypeStruct((count, order, order), BF16),
        cost_estimate=pl.CostEstimate(
            flops=flops, bytes_accessed=4 * count * order * order + 4 * count * surface**2, transcendentals=0
        ),
        name="sandwich",
    )(green, left_in, right_in, grad, lc, rc)


def phonon_kernel(high, scale, rows, n_sand, n_green, *refs):
    shifts_ref, place_ref = refs[0], refs[1]
    sands = refs[2 : 2 + n_sand]
    greens = refs[2 + n_sand : 2 + n_sand + n_green]
    keep_ref, send_ref, sand_buf, green_buf, sand_sem, green_sem = refs[2 + n_sand + n_green :]
    order = keep_ref.shape[-1]
    chips = keep_ref.shape[0]
    blocks = order // rows
    count = sands[-1].shape[0] + (sands[-2].shape[0] if n_sand > 2 else 0)

    def copies(block):
        window = pl.ds(pl.multiple_of(block * rows, rows), rows)
        made, at = [], 0
        for index, ref in enumerate(sands):
            made.append(
                pltpu.make_async_copy(
                    ref.at[:, window, :],
                    sand_buf.at[pl.ds(at, ref.shape[0]), window, :],
                    sand_sem.at[index, block],
                )
            )
            at += ref.shape[0]
        at = 0
        for index, ref in enumerate(greens):
            made.append(
                pltpu.make_async_copy(
                    ref.at[:, window, :],
                    green_buf.at[pl.ds(at, ref.shape[0]), window, :],
                    green_sem.at[index, block],
                )
            )
            at += ref.shape[0]
        return made

    for block in range(blocks):
        for copy in copies(block):
            copy.start()
    place = place_ref[0]
    chip, core = place // 2, lax.rem(place, 2)
    energies = green_buf.shape[0] if n_green == 1 else greens[0].shape[0]

    def one_block(block, carry):
        for copy in copies(block):
            copy.wait()
        window = pl.ds(pl.multiple_of(block * rows, rows), rows)

        def one_term(term, carry):
            offset = lax.rem(term, chips)
            side = term // chips
            which = 2 * (chip ^ offset) + (core ^ side)
            shift = shifts_ref[which]
            back = jnp.minimum(shift, high)
            first_s = high - back
            first_g = shift - back
            total = jnp.zeros((rows, order), F32)
            for t in range(0, energies, 4):
                p = [
                    sand_buf[first_s + t + u, window, :] * green_buf[first_g + t + u, window, :]
                    for u in range(4)
                ]
                total = total + ((p[0] + p[1]) + (p[2] + p[3])).astype(F32)
            total = (total * scale).astype(BF16)

            @pl.when(side == 0)
            def _():
                keep_ref[offset, window, :] = total

            @pl.when(side == 1)
            def _():
                send_ref[offset, window, :] = total

            return carry

        return lax.fori_loop(0, 2 * chips, one_term, carry)

    lax.fori_loop(0, blocks, one_block, 0)


def phonon_partials(shifts, place, sands, greens, high, scale, rows):
    order = sands[0].shape[-1]
    half = shifts.shape[0] // 2
    sand_total = sum(s.shape[0] for s in sands)
    green_total = sum(g.shape[0] for g in greens)
    blocks = order // rows
    return pl.pallas_call(
        functools.partial(phonon_kernel, high, scale, rows, len(sands), len(greens)),
        in_specs=[SMEM, SMEM] + [ANY] * (len(sands) + len(greens)),
        out_specs=(VMEM, VMEM),
        out_shape=(
            jax.ShapeDtypeStruct((half, order, order), BF16),
            jax.ShapeDtypeStruct((half, order, order), BF16),
        ),
        scratch_shapes=[
            pltpu.VMEM((sand_total, order, order), BF16),
            pltpu.VMEM((green_total, order, order), BF16),
            pltpu.SemaphoreType.DMA((len(sands), blocks)),
            pltpu.SemaphoreType.DMA((len(greens), blocks)),
        ],
        cost_estimate=pl.CostEstimate(
            flops=2 * shifts.shape[0] * greens[0].shape[0] * order * order,
            bytes_accessed=2 * (sand_total + green_total) * order * order,
            transcendentals=0,
        ),
        name="phonon",
    )(shifts, place, *sands, *greens)


def add_kernel(a_ref, b_ref, *outs):
    for index, out in enumerate(outs):
        out[...] = (a_ref[index + 1].astype(F32) + b_ref[index + 1].astype(F32)).astype(BF16)


def pair_sums(keep, recv):
    chips, order = keep.shape[0], keep.shape[-1]
    return pl.pallas_call(
        add_kernel,
        in_specs=[VMEM, VMEM],
        out_specs=tuple([VMEM] * (chips - 1)),
        out_shape=tuple([jax.ShapeDtypeStruct((order, order), BF16)] * (chips - 1)),
        name="pairsum",
    )(keep, recv)


def full_dot(a, b):
    return lax.dot_general(
        a, b, (((1,), (0,)), ((), ())), precision=lax.Precision.HIGHEST, preferred_element_type=F32
    )


def invert_kernel(n_pieces, *refs):
    omega_ref, place_ref, keep_ref, recv_ref = refs[:4]
    pieces = refs[4 : 4 + n_pieces]
    stiff_ref, self_ref, inverse_ref, rounded_ref = refs[4 + n_pieces :]
    order = stiff_ref.shape[-1]
    total = keep_ref[...].astype(F32) + recv_ref[...].astype(F32)
    for piece in pieces:
        total = total + piece[...].astype(F32)
    self_ref[...] = total
    row = lax.broadcasted_iota(jnp.int32, (order, order), 0)
    column = lax.broadcasted_iota(jnp.int32, (order, order), 1)
    on = row == column
    omega = omega_ref[place_ref[0]]
    matrix = stiff_ref[...] + jnp.where(on, omega, 0.0) + coupling * total
    picked = jnp.where(on, matrix, 0.0)
    across = 1.0 / jnp.sum(picked, axis=0, keepdims=True)
    down = 1.0 / jnp.sum(picked, axis=1, keepdims=True)
    approx = jnp.where(on, 2.0 * across, 0.0) - down * (matrix * across)
    for repeat in range(NEWTON - 1):
        product = full_dot(matrix, approx)
        approx = 2.0 * approx - full_dot(approx, product)
    inverse_ref[...] = approx
    rounded_ref[...] = approx.astype(BF16)


def inverted(omega_sq, place, keep, recv, pieces, stiffness):
    order = stiffness.shape[-1]
    head = pl.BlockSpec((None, order, order), lambda i: (0, 0, 0))
    flat = pl.BlockSpec((order, order), lambda i: (0, 0))
    wide = pl.BlockSpec((None, None, order, order), lambda i: (0, 0, 0, 0))
    return pl.pallas_call(
        functools.partial(invert_kernel, len(pieces)),
        grid=(1,),
        in_specs=[SMEM, SMEM, head, head] + [flat] * len(pieces) + [head],
        out_specs=(wide, wide, flat),
        out_shape=(
            jax.ShapeDtypeStruct((1, 1, order, order), F32),
            jax.ShapeDtypeStruct((1, 1, order, order), F32),
            jax.ShapeDtypeStruct((order, order), BF16),
        ),
        name="inverse",
    )(omega_sq, place, keep, recv, *pieces, stiffness)


def mixture_kernel(rows, n_sand, n_freq, *refs):
    shifts_ref, place_ref = refs[0], refs[1]
    sands = refs[2 : 2 + n_sand]
    freqs = refs[2 + n_sand : 2 + n_sand + n_freq]
    grad_ref, out_ref, sand_buf, half_buf, out_buf, sand_sem, out_sem = refs[2 + n_sand + n_freq :]
    count, order = out_buf.shape[0], out_buf.shape[-1]
    blocks = order // rows

    def copies(block):
        window = pl.ds(pl.multiple_of(block * rows, rows), rows)
        made, at = [], 0
        for index, ref in enumerate(sands):
            made.append(
                pltpu.make_async_copy(
                    ref.at[:, window, :],
                    sand_buf.at[pl.ds(at, ref.shape[0]), window, :],
                    sand_sem.at[index, block],
                )
            )
            at += ref.shape[0]
        return made

    for block in range(blocks):
        for copy in copies(block):
            copy.start()
    place = place_ref[0]
    firsts = [count - shifts_ref[place ^ index] for index in range(n_freq)]
    grad = grad_ref[...]

    def one_block(block, carry):
        for copy in copies(block):
            copy.wait()
        window = pl.ds(pl.multiple_of(block * rows, rows), rows)
        weights = [freq[window, :] for freq in freqs]

        def some(step, carry):
            pieces = []
            for u in range(4):
                e = step * 4 + u
                terms = [
                    weights[k] * sand_buf[firsts[k] + e, window, :] for k in range(n_freq)
                ]
                while len(terms) > 2:
                    terms = [terms[k] + terms[k + 1] for k in range(0, len(terms), 2)]
                pieces.append((terms[0].astype(F32) + terms[1].astype(F32)).astype(BF16))
            mixed = jnp.concatenate(pieces, axis=0)
            half = dot_nt(mixed, grad).astype(BF16)
            for u in range(4):
                half_buf[step * 4 + u, window, :] = half[u * rows : (u + 1) * rows]
            return carry

        return lax.fori_loop(0, count // 4, some, carry)

    lax.fori_loop(0, blocks, one_block, 0)

    def finish(e):
        return pltpu.make_async_copy(out_buf.at[e], out_ref.at[e, 0], out_sem.at[e])

    def one_energy(step, carry):
        for u in range(4):
            e = step * 4 + u
            out_buf[e] = dot_nn(grad, half_buf[e]).astype(BF16)
            finish(e).start()
        return carry

    lax.fori_loop(0, count // 4, one_energy, 0)
    for e in range(count):
        finish(e).wait()


def electron_of(shifts, place, sands, freqs, grad, rows):
    order = sands[0].shape[-1]
    sand_total = sum(s.shape[0] for s in sands)
    count = sand_total // 2
    blocks = order // rows
    return pl.pallas_call(
        functools.partial(mixture_kernel, rows, len(sands), len(freqs)),
        grid=(1,),
        in_specs=[SMEM, SMEM]
        + [ANY] * len(sands)
        + [pl.BlockSpec((order, order), lambda i: (0, 0))] * len(freqs)
        + [pl.BlockSpec((None, order, order), lambda i: (0, 0, 0))],
        out_specs=ANY,
        out_shape=jax.ShapeDtypeStruct((count, 1, order, order), BF16),
        scratch_shapes=[
            pltpu.VMEM((sand_total, order, order), BF16),
            pltpu.VMEM((count, order, order), BF16),
            pltpu.VMEM((count, order, order), BF16),
            pltpu.SemaphoreType.DMA((len(sands), blocks)),
            pltpu.SemaphoreType.DMA((count,)),
        ],
        cost_estimate=pl.CostEstimate(
            flops=4 * count * order**3, bytes_accessed=6 * count * order * order, transcendentals=0
        ),
        name="mixture",
    )(shifts, place, *sands, *freqs, grad)


def body(green, gradient, left_coupling, right_coupling, dynamical, omega_sq, shifts):
    per_device = green.shape[0]
    order = green.shape[-1]
    surface = left_coupling.shape[-1]
    groups = lax.axis_size("energy")
    chips = groups // 2
    scale = 1.0 / math.sqrt(per_device * groups)
    place = lax.axis_index("energy").astype(jnp.int32).reshape(1)
    blocks = green[:, 0]
    left_in = shifted(blocks[:, order - surface :, order - surface :], "layer", 1)
    right_in = shifted(blocks[:, :surface, :surface], "layer", -1)
    sandwich = sandwich_of(
        green, 0, per_device, left_in, right_in, gradient, left_coupling, right_coupling, 4
    )
    lower = shifted(sandwich, "energy", 1)
    keep, send = phonon_partials(shifts, place, (lower, sandwich), (blocks,), per_device, scale, 32)
    recv = partner(send, "energy", 1)
    sums = pair_sums(keep, recv)
    pieces = [partner(sums[d - 1], "energy", 2 * d) for d in range(1, chips)]
    own_self, own_green, rounded = inverted(omega_sq, place, keep, recv, pieces, dynamical)
    freqs = [rounded] + [partner(rounded, "energy", d) for d in range(1, groups)]
    electron = electron_of(shifts, place, (lower, sandwich), freqs, gradient, 16)
    return (own_self, own_green, electron)


def solution(mesh):
    return jax.shard_map(
        body,
        mesh=mesh,
        in_specs=(
            P("energy", "layer", None, None),
            P("layer", None, None),
            P("layer", None, None),
            P("layer", None, None),
            P("layer", None, None),
            P(),
            P(),
        ),
        out_specs=(
            P("energy", "layer", None, None),
            P("energy", "layer", None, None),
            P("energy", "layer", None, None),
        ),
        check_vma=False,
    )
```
